1024 devices in a mesh: ctx: 8 (over y), mp: 128 (over z, x, core).
Axes of the slice: x: 8, y: 8, z: 8, core: 2. Of those that a mesh axis runs over, the one named last changes fastest.
Arguments:
- tokens: bfloat16 [1536, 8192], P('ctx'), may hold values from -120 to 120
- norm_gain: float32 [8192], replicated, may hold values from 0.1 to 1.9
- in_weight: bfloat16 [8192, 3, 8192], P(None, None, 'mp'), may hold values from -0.0625 to 0.0625
- short_filter: float32 [3, 3, 8192], P(None, None, 'mp'), may hold values from -3 to 3
- rates: float32 [16, 8192], P(None, 'mp'), may hold values from 6.510417e-05 to 0.020833334
- residues: float32 [16, 8192], P(None, 'mp'), may hold values from -4 to 4
- skip: float32 [8192], P('mp'), may hold values from -4 to 4
- out_weight: bfloat16 [8192, 8192], P('mp'), may hold values from -0.25 to 0.25
- segment_ids: int32 [1536], replicated, may hold values from 0 to 7, never falling along the last dimension, each value on 1 to 576 neighbouring positions
Outputs:
- mixed: bfloat16 [1536, 8192], P('ctx', 'mp')
The draws below stay inside these ranges and needn't reach their ends.
Inputs may be any that keep to these rules, and one draw needn't show every extreme that they name: `segment_ids`: never falls along the sequence; each document spans 1 to 576 positions.
All inputs are finite; a program needn't handle non-finite values.
Results may differ from the reference program's by a relative error of at most 0.0085.
Values may be sent and summed in bfloat16 or wider, within the bound.
A program may use at most 64 MiB of HBM per device.

```python
import math
import jax
import jax.numpy as jnp
import numpy as np
from jax import lax

D = 8192
ORDER = 16
KSHORT = 3
TOK_DEV = 192
SEQ = 1536
N_CTX = 8


def draw_tokens(key, part):
    key_rows, key_columns, key_values = jax.random.split(jax.random.fold_in(key, 11), 3)
    row_scale = jnp.exp(jax.random.uniform(key_rows, (SEQ, 1), minval=0.0, maxval=jnp.log(10.0)))
    column_scale = jnp.exp(jax.random.uniform(key_columns, (1, D), minval=jnp.log(0.3), maxval=jnp.log(3.0)))
    base = jnp.clip(jax.random.normal(key_values, (SEQ, D)), -4.0, 4.0)
    return (base * row_scale * column_scale).astype(jnp.float32).astype(jnp.bfloat16)


def spiked(values, rng, source, target, parts, factor):
    owner, partner = [(jnp.arange(values.shape[axis_at]) // (values.shape[axis_at] // parts)).reshape([-1 if axis == axis_at else 1 for axis in range(values.ndim)]) for axis_at in (source, target)]
    chosen = jax.random.permutation(rng, parts)[partner]
    strong = (owner == chosen) | (owner == (partner + parts // 2) % parts)
    return jnp.where(strong, factor * values, values)


def levels(key, extent, shards, least, high):
    loudness, own = 1.0, jax.random.fold_in(key, 6)
    for position, shards_of in shards:
        steps = jnp.exp(jax.random.uniform(jax.random.fold_in(own, position), (shards_of,), jnp.float32, least / len(shards), high / len(shards)))
        loudness = loudness * jnp.repeat(steps, extent[position] // shards_of).reshape([-1 if axis == position else 1 for axis in range(len(extent))])
    return loudness


def profile(number_of, total, limit, lean):
    loads = [(1 << 20) // math.isqrt(rank ** lean) + 1 for rank in range(2, number_of + 1)]
    surplus, holding = total - limit - (number_of - 1), [1] * (number_of - 1)
    while surplus > 0:
        candidates = [i for i in range(number_of - 1) if holding[i] < limit]
        mass, left = sum([loads[i] for i in candidates]), surplus
        for i in candidates:
            addition = min(limit - holding[i], max(1, left * loads[i] // mass), surplus)
            holding[i] = holding[i] + addition
            surplus = surplus - addition
    return np.array([limit] + holding)


def ragged_sizes(stream_key, amount, total, reach, lean):
    if amount == 2:
        one = jax.random.randint(stream_key, (), max(1, total - reach), min(reach, total - 1) + 1)
        return jnp.stack([one, total - one])
    lengths = jnp.asarray(profile(amount, total, reach, lean), jnp.int32)
    twos = (amount - 1) // 2
    source_of, taker = lengths[1:1 + 2 * twos:2], lengths[2:2 + 2 * twos:2]
    room = jnp.minimum(source_of - 1, reach - taker)
    passed = jax.random.randint(jax.random.fold_in(stream_key, 1), (twos,), 0, 1 << 20) % (room + 1)
    lengths = lengths.at[1:1 + 2 * twos:2].set(source_of - passed).at[2:2 + 2 * twos:2].set(taker + passed)
    return lengths[jax.random.permutation(jax.random.fold_in(stream_key, 2), amount)]


def normal_values(rng, shape, spread, most, pieces=(), held_as=jnp.bfloat16):
    gain = levels(rng, shape, pieces, -0.22, 0.18) if pieces else 1.0
    values = jax.random.normal(rng, shape, jnp.float32) * spread * gain
    return jnp.minimum(jnp.maximum(values, -most), most).astype(held_as)


def heavy_noise(rng, dims, spread, bound, pieces, heavy, kind=jnp.bfloat16):
    result = spread * jax.random.normal(rng, dims, jnp.float32)
    if pieces:
        result = result * levels(rng, dims, pieces, -0.22, 0.18)
    return jnp.clip(spiked(result, jax.random.fold_in(rng, 3), *heavy), -bound, bound).astype(kind)


def setup_inputs(seed: int = 0) -> dict:
    key_of = jax.random.split(jax.random.key(seed), 10)
    tokens = draw_tokens(jax.random.fold_in(key_of[9], 71), 0)
    norm_gain = jnp.clip(1.0 + 0.18 * jax.random.normal(key_of[1], (D,), jnp.float32), 0.1, 1.9)
    in_weight = normal_values(key_of[2], (D, 3, D), D ** -0.5, 0.0625, ((2, 128),))
    short_filter = normal_values(key_of[3], (KSHORT, 3, D), 0.5, 3.0, ((2, 128),), jnp.float32)
    rates = jnp.clip(jnp.exp(math.log(0.020833334) - 5.768321 * jax.random.uniform(key_of[4], (ORDER, D), jnp.float32) ** levels(key_of[4], (ORDER, D), ((1, 128),), -0.2, 0.2)), 6.510417006211355e-05, 0.020833334)
    residues = normal_values(key_of[5], (ORDER, D), (ORDER ** -0.5), 4.0, ((1, 128),), jnp.float32)
    skip = normal_values(key_of[6], (D,), 1.0, 4.0, ((0, 128),), jnp.float32)
    out_weight = heavy_noise(key_of[7], (D, D), D ** -0.5, 0.25, ((0, 128),), (0, 1, 128, 5.5))
    segment_ids = jnp.searchsorted(jnp.cumsum(ragged_sizes(key_of[8], N_CTX, SEQ, 3 * TOK_DEV, 1)), jnp.arange(SEQ), side="right").astype(jnp.int32)
    return dict(tokens=tokens, norm_gain=norm_gain, in_weight=in_weight, short_filter=short_filter, rates=rates, residues=residues, skip=skip, out_weight=out_weight, segment_ids=segment_ids)


epsilon = 1e-06

def reference(tokens, norm_gain, in_weight, short_filter, rates, residues, skip, out_weight, segment_ids):
    floats = tokens.astype(jnp.float32)
    mean_square = lax.optimization_barrier(jnp.mean(floats * floats, axis=-1, keepdims=True))
    normed = (floats * lax.rsqrt(mean_square + epsilon) * norm_gain[None, :]).astype(jnp.bfloat16)
    projected = jnp.dot(normed, in_weight.reshape(D, 3 * D), preferred_element_type=jnp.float32)
    projected = projected.astype(jnp.bfloat16).reshape(SEQ, 3, D)
    featured = jnp.zeros((SEQ, 3, D), jnp.float32)
    for lag_index in range(KSHORT):
        lagged = jnp.concatenate([jnp.zeros((lag_index, 3, D), jnp.bfloat16), projected[:SEQ - lag_index]], axis=0)
        lagged_ids = jnp.concatenate([jnp.full((lag_index,), -1, jnp.int32), segment_ids[:SEQ - lag_index]], axis=0)
        matches = segment_ids == lagged_ids
        term = short_filter[lag_index][None] * lagged.astype(jnp.float32)
        featured = featured + jnp.where(matches[:, None, None], term, jnp.zeros_like(term))
    query_part = featured[:, 0]
    key_part = featured[:, 1]
    value_part = featured[:, 2]
    product = key_part * value_part
    decay = jnp.exp(-rates)
    pole_weight = residues * jnp.sqrt(-jnp.expm1(-2.0 * rates))
    keeping = jnp.concatenate([jnp.zeros((1,), bool), segment_ids[1:] == segment_ids[:-1]], axis=0)

    def advance(state, inputs):
        product_row, keep_row = inputs
        state = jnp.where(keep_row, decay * state, jnp.zeros_like(state)) + product_row[None, :]
        return (state, lax.optimization_barrier(jnp.sum(pole_weight * state, axis=0)))
    _, longconv = lax.scan(advance, jnp.zeros((ORDER, D), jnp.float32), (product, keeping))
    gated = (query_part * (longconv + skip[None, :] * product)).astype(jnp.bfloat16)
    return jnp.dot(gated, out_weight, preferred_element_type=jnp.float32).astype(jnp.bfloat16)
```

```python
import functools

import jax
import jax.numpy as jnp
from jax import lax
from jax.experimental import pallas as pl
from jax.experimental.pallas import tpu as pltpu
from jax.sharding import Mesh
from jax.sharding import PartitionSpec as P

MP = ("mp_0", "mp_1", "mp_2")
MESH = pl.DeviceIdType.MESH
F32 = jnp.float32
BF16 = jnp.bfloat16

epsilon = 1e-06

ROWS = 192
HALF = ROWS // 2
QUARTER = HALF // 2
CH = 64
POLES = 16
PAIRS = POLES // 2
WIDTH = 8192
DOCS = 8
CENTER = float(ROWS // 2)
CLASSES = 4
TOKEN_CHUNK = 2048
WEIGHT_CHUNK = 1024


def distances(count):
    return sorted(range(1, count), key=lambda d: -min(d, count - d))


def kernel(
    sizes,
    tokens, gain, in_weight, taps, rates, residues, skip, out_weight, ids,
    out,
    tok, win, wout, proj, halo, growth, weighted, visible, product, query, acc,
    lag_one, lag_two, survives, ends, incoming, a_send, a_recv, lhs, c_send, c_recv,
    tok_sem, win_sem, s1_send, s1_recv, s2_send, s2_recv, oc_send, oc_recv,
    halo_sem, e_send, e_recv, as_sem, ar_sem, cs_sem, cr_sem,
):
    ny, nz, nx = sizes
    y, z, x, c = (lax.axis_index(name) for name in ("ctx", *MP))
    other = 1 - c
    per_class = nz // CLASSES
    group = nx * CH

    def at_y(step):
        return (lax.rem(y + step + ny, ny), z, x, c)

    tok_loads = []
    for k in range(WIDTH // TOKEN_CHUNK):
        span = pl.ds(k * TOKEN_CHUNK, TOKEN_CHUNK)
        load = pltpu.make_async_copy(tokens.at[:, span], tok.at[:, span], tok_sem.at[k])
        load.start()
        tok_loads.append(load)
    win_loads = []
    for k in range(WIDTH // WEIGHT_CHUNK):
        span = pl.ds(k * WEIGHT_CHUNK, WEIGHT_CHUNK)
        for part, (source, target, count) in enumerate(((0, 0, 3 * CH), (2 * CH, 3 * CH, CH))):
            load = pltpu.make_async_copy(
                in_weight.at[pl.ds(source, count), span],
                win.at[pl.ds(target, count), span],
                win_sem.at[2 * k + part],
            )
            load.start()
            win_loads.append(load)

    barrier = pltpu.get_barrier_semaphore()
    greeted = [(y, z, x, other)]
    for parity in (c, other):
        greeted += [(y, z, lax.rem(x + d, nx), parity) for d in range(1, nx)]
        greeted += [(y, lax.rem(z + d, nz), x, parity) for d in range(1, nz)]
    steps = sorted({d % ny for d in (1, 2, 3, -1, -2, -3)})
    greeted += [at_y(d) for d in steps]
    for device in greeted:
        pl.semaphore_signal(barrier, inc=1, device_id=device, device_id_type=MESH)

    id_values = ids[...].astype(F32)
    bounds = [
        jnp.sum(jnp.where(id_values < float(k), 1.0, 0.0), axis=(0, 1), keepdims=True)
        for k in range(1, DOCS)
    ]

    def document(position):
        total = jnp.zeros_like(position)
        for bound in bounds:
            total = total + jnp.where(position >= bound, 1.0, 0.0)
        return total

    base = (y * ROWS).astype(F32)
    down = lax.broadcasted_iota(jnp.int32, (ROWS, 128), 0).astype(F32)
    own = document(down + base)

    def document_at(offset):
        return document(jnp.zeros((1, 128), F32) + (base + float(offset)))

    before = [document_at(-1 - ROWS * k) for k in range(3)]
    reach = [jnp.where(y >= k, 1.0, 0.0).astype(F32) for k in range(4)]
    survives[...] = jnp.where(own == before[0], reach[1], 0.0)
    lag_one[...] = jnp.where(own == document(down + (base - 1.0)), 1.0, 0.0)
    lag_two[...] = jnp.where(own == document(down + (base - 2.0)), 1.0, 0.0)
    whole = jnp.where(document_at(0) == document_at(ROWS - 1), 1.0, 0.0)
    across = lax.broadcasted_iota(jnp.int32, (1, 2 * ROWS), 1).astype(F32)
    across = jnp.where(across < float(ROWS), across, across - float(ROWS))
    beside = document(across + base)
    seen = (down[:, :1] >= across) & (own[:, :1] == beside)
    visible[...] = jnp.where(seen, 1.0, 0.0).astype(BF16)

    def paired(ref):
        return jnp.concatenate([ref[0:PAIRS, :], ref[PAIRS:POLES, :]], axis=1)

    rate = paired(rates)
    twice = -2.0 * rate
    small = twice * (1.0 + twice * (0.5 + twice * (1.0 / 6.0 + twice * (1.0 / 24.0 + twice * (
        1.0 / 120.0)))))
    weight = paired(residues) * jnp.sqrt(-small)

    squares = jnp.zeros((ROWS, 128), F32)
    for k in range(WIDTH // TOKEN_CHUNK):
        tok_loads[k].wait()
        for lane in range(k * TOKEN_CHUNK, (k + 1) * TOKEN_CHUNK, 128):
            piece = tok[:, lane : lane + 128].astype(F32)
            squares = squares + piece * piece
    mean_square = jnp.sum(squares, axis=1, keepdims=True) * (1.0 / WIDTH)
    scale = lax.rsqrt(mean_square + epsilon)

    pl.semaphore_wait(barrier, len(greeted))

    kind = lax.rem(y, CLASSES)

    def block(j, turned=0):
        return lax.rem(kind + turned + CLASSES, CLASSES) + CLASSES * j

    def columns(index):
        return pl.ds(pl.multiple_of(index * 128, 128), 128)

    mine = pl.ds(pl.multiple_of(c * group + x * CH, CH), CH)
    s1 = []
    for j in range(per_class):
        for i, d in enumerate(distances(nx)):
            there = lax.rem(x + d, nx)
            copy = pltpu.make_async_remote_copy(
                src_ref=out_weight.at[:, columns(block(j) * nx + there)],
                dst_ref=wout.at[mine, columns(block(j))],
                send_sem=s1_send.at[j * nx + i],
                recv_sem=s1_recv.at[j * nx + x],
                device_id=(y, z, there, c),
                device_id_type=MESH,
            )
            copy.start()
            s1.append(copy)
    kept = [
        pltpu.make_async_copy(
            out_weight.at[:, columns(block(j) * nx + x)],
            wout.at[mine, columns(block(j))],
            s1_recv.at[j * nx + x],
        )
        for j in range(per_class)
    ]
    for copy in kept:
        copy.start()

    acc[...] = jnp.zeros_like(acc)
    for k in range(WIDTH // WEIGHT_CHUNK):
        win_loads[2 * k].wait()
        win_loads[2 * k + 1].wait()
        span = pl.ds(k * WEIGHT_CHUNK, WEIGHT_CHUNK)
        normed = (tok[:, span].astype(F32) * scale * gain[:, span]).astype(BF16)
        acc[...] += lax.dot_general(
            normed, win[:, span], (((1,), (1,)), ((), ())), preferred_element_type=F32
        )
    proj[0:8, :] = jnp.zeros((8, 256), F32)
    proj[8 : 8 + ROWS, :] = acc[...].astype(BF16).astype(F32)
    halo_copy = pltpu.make_async_remote_copy(
        src_ref=proj.at[pl.ds(ROWS, 8)],
        dst_ref=halo,
        send_sem=halo_sem.at[0],
        recv_sem=halo_sem.at[1],
        device_id=at_y(1),
        device_id_type=MESH,
    )
    halo_copy.start()

    def is_low(count):
        return lax.broadcasted_iota(jnp.int32, (count, 128), 1) < CH

    tap_rows = []
    for j in range(3):
        first = jnp.concatenate([taps[j, 0:1, :], taps[j, 1:2, :]], axis=1)
        second = jnp.concatenate([taps[j, 2:3, :], taps[j, 2:3, :]], axis=1)
        tap_rows.append((first, second))

    def filtered(count):
        tiles = []
        for side in range(2):
            lanes = slice(128 * side, 128 * side + 128)
            total = tap_rows[0][side] * proj[8 : 8 + count, lanes]
            total = total + tap_rows[1][side] * (proj[7 : 7 + count, lanes] * lag_one[0:count, :])
            total = total + tap_rows[2][side] * (proj[6 : 6 + count, lanes] * lag_two[0:count, :])
            tiles.append(total)
        turned = pltpu.roll(tiles[0], CH, 1)
        side = is_low(count)
        return jnp.where(side, tiles[0], turned), jnp.where(side, turned, tiles[0]) * tiles[1]

    query_part, product_part = filtered(ROWS)
    query[...] = query_part
    product[...] = product_part

    offset = down - CENTER
    for g in range(PAIRS):
        lanes = slice(128 * g, 128 * g + 128)
        exponent = offset * rate[g : g + 1, :]
        value = jnp.exp(exponent) * product_part
        high = value.astype(BF16)
        weighted[0:ROWS, lanes] = high
        weighted[ROWS : 2 * ROWS, lanes] = (value - high.astype(F32)).astype(BF16)
        growth[:, lanes] = weight[g : g + 1, :] * jnp.exp(-exponent)
    last = []
    total = jnp.zeros((ROWS, 128), F32)
    for g in range(PAIRS):
        lanes = slice(128 * g, 128 * g + 128)
        inside = jnp.dot(visible[...], weighted[:, lanes], preferred_element_type=F32)
        last.append(inside[ROWS - 1 : ROWS, :])
        total = total + growth[:, lanes] * inside
    last = jnp.concatenate(last, axis=0)

    halo_copy.wait_recv()
    proj[0:8, :] = halo[...] * reach[1]
    query_top, product_top = filtered(8)
    change = product_top - product[0:8, :]
    query[0:8, :] = query_top
    product[0:8, :] = product_top
    change_zero = jnp.exp(-CENTER * rate) * change[0:1, :]
    change_one = jnp.exp((1.0 - CENTER) * rate) * change[1:2, :]
    ends[...] = jnp.exp((CENTER + 1.0 - ROWS) * rate) * (
        last + whole * (change_zero + change_one)
    )
    e_copies = []
    for k in range(3):
        copy = pltpu.make_async_remote_copy(
            src_ref=ends,
            dst_ref=incoming.at[k],
            send_sem=e_send.at[k],
            recv_sem=e_recv.at[k],
            device_id=at_y(k + 1),
            device_id_type=MESH,
        )
        copy.start()
        e_copies.append(copy)

    parity = pl.ds(pl.multiple_of(c * group, group), group)

    def passed_on(index, sem, target):
        return pltpu.make_async_remote_copy(
            src_ref=wout.at[parity, columns(index)],
            dst_ref=wout.at[parity, columns(index)],
            send_sem=s2_send.at[sem],
            recv_sem=s2_recv.at[sem],
            device_id=target,
            device_id_type=MESH,
        )

    def handed(index):
        return pltpu.make_async_remote_copy(
            src_ref=wout.at[parity, columns(index)],
            dst_ref=wout.at[parity, columns(index)],
            send_sem=oc_send.at[index],
            recv_sem=oc_recv.at[index],
            device_id=(y, z, x, other),
            device_id_type=MESH,
        )

    for j in range(per_class):
        for d in range(1, nx):
            there = lax.rem(x + d, nx)
            pltpu.make_async_copy(
                wout.at[mine, columns(block(j))],
                wout.at[mine, columns(block(j))],
                s1_recv.at[j * nx + there],
            ).wait()
        kept[j].wait()
    s2 = []
    handovers = []
    half_class = per_class // 2
    rightward = list(range(per_class))
    leftward = rightward[half_class:] + rightward[:half_class]
    for j, k in zip(rightward, leftward):
        for copy in (
            passed_on(block(j), j, at_y(1)),
            passed_on(block(k), per_class + k, at_y(-1)),
        ):
            copy.start()
            s2.append(copy)
    for j in range(per_class):
        copy = handed(block(j))
        copy.start()
        handovers.append(copy)

    for k in range(3):
        e_copies[k].wait_recv()
    carried = reach[1] * incoming[0]
    for k in (1, 2):
        reached = jnp.where(before[0] == before[k], reach[k + 1], 0.0)
        carried = carried + reached * jnp.exp(-float(ROWS * k) * rate) * incoming[k]
    carried = jnp.exp(-(CENTER + 1.0) * rate) * carried + change_zero
    entering = jnp.zeros((ROWS, 128), F32)
    changed = jnp.zeros((ROWS, 128), F32)
    for g in range(PAIRS):
        lanes = slice(128 * g, 128 * g + 128)
        entering = entering + growth[:, lanes] * carried[g : g + 1, :]
        changed = changed + growth[:, lanes] * change_one[g : g + 1, :]
    total = total + survives[...] * (entering + jnp.where(down >= 1.0, changed, 0.0))
    total = total + pltpu.roll(total, CH, 1)
    skips = jnp.concatenate([skip[...], skip[...]], axis=1)
    gated = query[...] * (total + skips * product[...])
    side = is_low(QUARTER)
    for h in range(2):
        top = gated[HALF * h : HALF * h + QUARTER, :]
        bottom = gated[HALF * h + QUARTER : HALF * (h + 1), :]
        a_send[h] = jnp.where(side, top, bottom).astype(BF16)

    a_copies = []

    def gather(i, there, target):
        copy = pltpu.make_async_remote_copy(
            src_ref=a_send.at[target],
            dst_ref=a_recv.at[c * nx + x],
            send_sem=as_sem.at[i],
            recv_sem=ar_sem.at[c * nx + x],
            device_id=(y, z, there, target),
            device_id_type=MESH,
        )
        copy.start()
        a_copies.append(copy)

    for i, d in enumerate(distances(nx)):
        there = lax.rem(x + d, nx)
        gather(2 * i, there, c)
        gather(2 * i + 1, there, other)
    gather(2 * nx - 2, x, other)
    a_recv[c * nx + x] = a_send[c]

    def arrived(index, sem):
        pltpu.make_async_copy(
            wout.at[parity, columns(index)], wout.at[parity, columns(index)], s2_recv.at[sem]
        ).wait()

    def hand(index):
        copy = handed(index)
        copy.start()
        handovers.append(copy)

    far = 2 * per_class
    for j in range(half_class):
        k = j + half_class
        arrived(block(j, -1), j)
        copy = passed_on(block(j, -1), far + j, at_y(1))
        copy.start()
        s2.append(copy)
        arrived(block(k, 1), per_class + k)
        copy = passed_on(block(k, 1), far + k, at_y(-1))
        copy.start()
        s2.append(copy)
        hand(block(j, -1))
        hand(block(k, 1))
    for j in range(half_class):
        k = j + half_class
        arrived(block(k, -1), k)
        hand(block(k, -1))
        arrived(block(j, 1), per_class + j)
        hand(block(j, 1))

    for d in range(1, 2 * nx):
        sender = lax.rem(c * nx + x + d, 2 * nx)
        pltpu.make_async_copy(a_recv.at[0], a_recv.at[0], ar_sem.at[sender]).wait()
    for m in range(nx):
        left = a_recv[2 * m].astype(F32)
        right = a_recv[2 * m + 1].astype(F32)
        lanes = slice(128 * m, 128 * m + 128)
        lhs[0:QUARTER, lanes] = jnp.where(side, left, pltpu.roll(right, CH, 1)).astype(BF16)
        lhs[QUARTER:HALF, lanes] = jnp.where(side, pltpu.roll(left, CH, 1), right).astype(BF16)

    for j in range(half_class):
        k = j + half_class
        arrived(block(j, 2), far + j)
        hand(block(j, 2))
        arrived(block(k, 2), far + k)
        hand(block(k, 2))
    partner = pl.ds(pl.multiple_of(other * group, group), group)
    for index in range(nz):
        pltpu.make_async_copy(
            wout.at[partner, columns(index)], wout.at[partner, columns(index)], oc_recv.at[index]
        ).wait()

    c_copies = []

    def scatter(i, slot, there, target):
        copy = pltpu.make_async_remote_copy(
            src_ref=c_send.at[slot, target],
            dst_ref=c_recv.at[c * nz + z],
            send_sem=cs_sem.at[i],
            recv_sem=cr_sem.at[c * nz + z],
            device_id=(y, there, x, target),
            device_id_type=MESH,
        )
        copy.start()
        c_copies.append(copy)

    for i, d in enumerate([*distances(nz), 0]):
        there = lax.rem(z + d, nz)
        sums = jnp.dot(lhs[...], wout[:, columns(there)], preferred_element_type=F32)
        top, bottom = sums[0:QUARTER, :], sums[QUARTER:HALF, :]
        c_send[i, 0] = jnp.where(side, top, pltpu.roll(bottom, CH, 1)).astype(BF16)
        c_send[i, 1] = jnp.where(side, pltpu.roll(top, CH, 1), bottom).astype(BF16)
        if d:
            scatter(2 * i, i, there, c)
            scatter(2 * i + 1, i, there, other)
        else:
            scatter(2 * i, i, there, other)
            c_recv[c * nz + z] = c_send[i, c]
    for d in range(1, 2 * nz):
        sender = lax.rem(c * nz + z + d, 2 * nz)
        pltpu.make_async_copy(c_recv.at[0], c_recv.at[0], cr_sem.at[sender]).wait()
    pieces = []
    for h in range(2):
        added = c_recv[h * nz].astype(F32)
        for k in range(1, nz):
            added = added + c_recv[h * nz + k].astype(F32)
        pieces += [added, pltpu.roll(added, CH, 1)]
    result = jnp.concatenate(pieces, axis=0)
    out[...] = result.T[0:CH, :].astype(BF16)

    for copy in (*s1, *s2, *handovers, *e_copies, *a_copies, *c_copies):
        copy.wait_send()
    halo_copy.wait_send()


def local(
    sizes,
    tokens, norm_gain, in_weight, short_filter, rates, residues, skip, out_weight, segment_ids,
):
    ny, nz, nx = sizes
    width = tokens.shape[1]
    turned = jnp.transpose(in_weight, (1, 2, 0)).reshape(3 * CH, width)
    per_class = nz // CLASSES
    vmem, hbm = pl.BlockSpec(memory_space=pltpu.VMEM), pl.BlockSpec(memory_space=pl.ANY)
    dma = pltpu.SemaphoreType.DMA
    result = pl.pallas_call(
        functools.partial(kernel, sizes),
        out_shape=jax.ShapeDtypeStruct((CH, ROWS), BF16),
        in_specs=[hbm, vmem, hbm, vmem, vmem, vmem, vmem, hbm, vmem],
        out_specs=vmem,
        scratch_shapes=[
            pltpu.VMEM((ROWS, WIDTH), BF16),
            pltpu.VMEM((4 * CH, WIDTH), BF16),
            pltpu.VMEM((2 * nx * CH, nz * 128), BF16),
            pltpu.VMEM((ROWS + 8, 256), F32),
            pltpu.VMEM((8, 256), F32),
            pltpu.VMEM((ROWS, PAIRS * 128), F32),
            pltpu.VMEM((2 * ROWS, PAIRS * 128), BF16),
            pltpu.VMEM((ROWS, 2 * ROWS), BF16),
            pltpu.VMEM((ROWS, 128), F32),
            pltpu.VMEM((ROWS, 128), F32),
            pltpu.VMEM((ROWS, 256), F32),
            pltpu.VMEM((ROWS, 128), F32),
            pltpu.VMEM((ROWS, 128), F32),
            pltpu.VMEM((ROWS, 128), F32),
            pltpu.VMEM((PAIRS, 128), F32),
            pltpu.VMEM((3, PAIRS, 128), F32),
            pltpu.VMEM((2, QUARTER, 128), BF16),
            pltpu.VMEM((2 * nx, QUARTER, 128), BF16),
            pltpu.VMEM((HALF, nx * 128), BF16),
            pltpu.VMEM((nz, 2, QUARTER, 128), BF16),
            pltpu.VMEM((2 * nz, QUARTER, 128), BF16),
            dma((WIDTH // TOKEN_CHUNK,)),
            dma((2 * WIDTH // WEIGHT_CHUNK,)),
            dma((per_class * nx,)),
            dma((per_class * nx,)),
            dma((3 * per_class,)),
            dma((3 * per_class,)),
            dma((nz,)),
            dma((nz,)),
            dma((2,)),
            dma((3,)),
            dma((3,)),
            dma((2 * nx,)),
            dma((2 * nx,)),
            dma((2 * nz,)),
            dma((2 * nz,)),
        ],
        compiler_params=pltpu.CompilerParams(
            collective_id=0, has_side_effects=True, vmem_limit_bytes=60 * 1024 * 1024
        ),
    )(
        tokens,
        norm_gain.reshape(1, width),
        turned,
        short_filter,
        rates,
        residues,
        skip.reshape(1, CH),
        out_weight,
        segment_ids.reshape(-1, 128),
    )
    return result.T


def solution(mesh):
    ny = mesh.shape["ctx"]
    nz, nx = 8, 8
    torus = Mesh(mesh.devices.reshape(ny, nz, nx, 2), ("ctx", *MP))
    placed = (
        P("ctx", None),
        P(),
        P(None, None, MP),
        P(None, None, MP),
        P(None, MP),
        P(None, MP),
        P(MP),
        P(MP, None),
        P(),
    )
    return jax.shard_map(
        functools.partial(local, (ny, nz, nx)),
        mesh=torus,
        in_specs=placed,
        out_specs=P("ctx", MP),
        check_vma=False,
    )
```

```python
import functools

import jax
import jax.numpy as jnp
from jax import lax
from jax.experimental import pallas as pl
from jax.experimental.pallas import tpu as pltpu
from jax.sharding import Mesh
from jax.sharding import PartitionSpec as P

MP = ("mp_0", "mp_1", "mp_2")
MESH = pl.DeviceIdType.MESH
F32 = jnp.float32
BF16 = jnp.bfloat16

epsilon = 1e-06

ROWS = 192
HALF = ROWS // 2
QUARTER = HALF // 2
CH = 64
POLES = 16
PAIRS = POLES // 2
WIDTH = 8192
DOCS = 8
CENTER = float(ROWS // 2)
REACH = 3
EARLY = 2
TOKEN_CHUNK = 2048
WEIGHT_CHUNK = 1024


def distances(count):
    return sorted(range(1, count), key=lambda d: -min(d, count - d))


def kernel(
    sizes,
    tokens, gain_in, in_weight, taps_in, rates_in, residues_in, skip_in, out_weight, ids_in,
    out,
    gain, taps, rates, residues, skip, ids, small_sem,
    tok, win, wout, proj, halo, growth, weighted, visible, product, query, acc,
    lag_one, lag_two, survives, ends, incoming, a_send, a_recv, lhs, sums, c_send, c_recv,
    tok_sem, win_sem, s1_send, s1_recv, s2_send, s2_recv, oc_send, oc_recv,
    halo_sem, e_send, e_recv, as_sem, ar_sem, cs_sem, cr_sem, z_ready,
):
    ny, nz, nx = sizes
    y, z, x, c = (lax.axis_index(name) for name in ("ctx", *MP))
    other = 1 - c
    def at_y(step):
        return (lax.rem(y + step + ny, ny), z, x, c)

    small = [
        pltpu.make_async_copy(source, target, small_sem.at[k])
        for k, (source, target) in enumerate(
            (
                (ids_in, ids),
                (rates_in, rates),
                (residues_in, residues),
                (taps_in, taps),
                (skip_in, skip),
                (gain_in, gain),
            )
        )
    ]
    for load in small:
        load.start()
    tok_loads = []
    for k in range(WIDTH // TOKEN_CHUNK):
        span = pl.ds(k * TOKEN_CHUNK, TOKEN_CHUNK)
        load = pltpu.make_async_copy(tokens.at[:, span], tok.at[:, span], tok_sem.at[k])
        load.start()
        tok_loads.append(load)

    barrier = pltpu.get_barrier_semaphore()
    greeted = [(y, z, x, other)]
    for side in (c, other):
        greeted += [(y, z, lax.rem(x + d, nx), side) for d in range(1, nx)]
    steps = sorted({d % ny for k in range(1, REACH + 1) for d in (k, -k)})
    greeted += [at_y(d) for d in steps]
    for device in greeted:
        pl.semaphore_signal(barrier, inc=1, device_id=device, device_id_type=MESH)
    for d in range(1, nz):

        @pl.when(z + d < nz)
        def _():
            for side in (c, other):
                target = (y, z + d, x, side)
                pl.semaphore_signal(barrier, inc=1, device_id=target, device_id_type=MESH)

    win_loads = []
    for k in range(WIDTH // WEIGHT_CHUNK):
        span = pl.ds(k * WEIGHT_CHUNK, WEIGHT_CHUNK)
        load = pltpu.make_async_copy(in_weight.at[:, span], win.at[:, span], win_sem.at[k])
        load.start()
        win_loads.append(load)
    for load in small:
        load.wait()

    id_values = ids[...].astype(F32)
    bounds = [
        jnp.sum(jnp.where(id_values < float(k), 1.0, 0.0), axis=(0, 1), keepdims=True)
        for k in range(1, DOCS)
    ]

    def document(position):
        total = jnp.zeros_like(position)
        for bound in bounds:
            total = total + jnp.where(position >= bound, 1.0, 0.0)
        return total

    base = (y * ROWS).astype(F32)
    down = lax.broadcasted_iota(jnp.int32, (ROWS, 128), 0).astype(F32)
    own = document(down + base)

    def document_at(offset):
        return document(jnp.zeros((1, 128), F32) + (base + float(offset)))

    before = [document_at(-1 - ROWS * k) for k in range(3)]
    reach = [jnp.where(y >= k, 1.0, 0.0).astype(F32) for k in range(4)]
    survives[...] = jnp.where(own == before[0], reach[1], 0.0)
    lag_one[...] = jnp.where(own == document(down + (base - 1.0)), 1.0, 0.0)
    lag_two[...] = jnp.where(own == document(down + (base - 2.0)), 1.0, 0.0)
    whole = jnp.where(document_at(0) == document_at(ROWS - 1), 1.0, 0.0)
    across = lax.broadcasted_iota(jnp.int32, (1, 2 * ROWS), 1).astype(F32)
    across = jnp.where(across < float(ROWS), across, across - float(ROWS))
    beside = document(across + base)
    seen = (down[:, :1] >= across) & (own[:, :1] == beside)
    visible[...] = jnp.where(seen, 1.0, 0.0).astype(BF16)

    def paired(ref):
        return jnp.concatenate([ref[0:PAIRS, :], ref[PAIRS:POLES, :]], axis=1)

    rate = paired(rates)
    twice = -2.0 * rate
    small = twice * (1.0 + twice * (0.5 + twice * (1.0 / 6.0 + twice * (1.0 / 24.0 + twice * (
        1.0 / 120.0)))))
    weight = paired(residues) * jnp.sqrt(-small)

    squares = jnp.zeros((ROWS, 128), F32)
    for k in range(WIDTH // TOKEN_CHUNK):
        tok_loads[k].wait()
        for lane in range(k * TOKEN_CHUNK, (k + 1) * TOKEN_CHUNK, 128):
            piece = tok[:, lane : lane + 128].astype(F32)
            squares = squares + piece * piece
    mean_square = jnp.sum(squares, axis=1, keepdims=True) * (1.0 / WIDTH)
    scale = lax.rsqrt(mean_square + epsilon)

    pl.semaphore_wait(barrier, len(greeted) + 2 * z)
    for d in range(1, nz):

        @pl.when(z - d >= 0)
        def _():
            for side in (c, other):
                target = (y, z - d, x, side)
                pl.semaphore_signal(
                    z_ready.at[c * nz + z], inc=1, device_id=target, device_id_type=MESH
                )

    mine = pl.ds(pl.multiple_of(c * CH, CH), CH)
    partner = pl.ds(pl.multiple_of(other * CH, CH), CH)

    width = nx * 128 // 2
    kind = lax.rem(y, 2)

    def columns(there, half):
        return pl.ds(pl.multiple_of((2 * there + half) * width, width), width)

    def place(index, half):
        return wout.at[index, mine, columns(0, half)]

    def spread(there):
        return pltpu.make_async_remote_copy(
            src_ref=out_weight.at[:, columns(there, kind)],
            dst_ref=place(z, kind),
            send_sem=s1_send.at[there],
            recv_sem=s1_recv.at[z],
            device_id=(y, there, x, c),
            device_id_type=MESH,
        )

    for half, sem in ((kind, s1_recv), (1 - kind, s2_recv)):
        pltpu.make_async_copy(
            out_weight.at[:, columns(z, half)], place(z, half), sem.at[z]
        ).start()
    for d in range(nz - 1, 0, -1):

        @pl.when(z - d >= 0)
        def _():
            spread(z - d).start()

    def wait_z(there, side):
        pl.semaphore_wait(z_ready.at[side * nz + there], 1)

    def spread_later(d):
        @pl.when(z + d < nz)
        def _():
            wait_z(z + d, c)
            spread(z + d).start()

    acc[...] = jnp.zeros_like(acc)
    for k in range(WIDTH // WEIGHT_CHUNK):
        win_loads[k].wait()
        span = pl.ds(k * WEIGHT_CHUNK, WEIGHT_CHUNK)
        normed = (tok[:, span].astype(F32) * scale * gain[:, span]).astype(BF16)
        acc[...] += lax.dot_general(
            normed, win[:, span], (((1,), (1,)), ((), ())), preferred_element_type=F32
        )
    proj[0:8, :] = jnp.zeros((8, 256), F32)
    rounded = acc[...].astype(BF16).astype(F32)
    proj[8 : 8 + ROWS, 0:128] = rounded[:, 0:128]
    value_part = rounded[:, 128 : 3 * CH]
    proj[8 : 8 + ROWS, 128:256] = jnp.concatenate([value_part, value_part], axis=1)
    halo_copy = pltpu.make_async_remote_copy(
        src_ref=proj.at[pl.ds(ROWS, 8)],
        dst_ref=halo,
        send_sem=halo_sem.at[0],
        recv_sem=halo_sem.at[1],
        device_id=at_y(1),
        device_id_type=MESH,
    )
    halo_copy.start()

    for d in range(1, EARLY + 1):
        spread_later(d)

    def is_low(count):
        return lax.broadcasted_iota(jnp.int32, (count, 128), 1) < CH

    tap_rows = []
    for j in range(3):
        first = jnp.concatenate([taps[j, 0:1, :], taps[j, 1:2, :]], axis=1)
        second = jnp.concatenate([taps[j, 2:3, :], taps[j, 2:3, :]], axis=1)
        tap_rows.append((first, second))

    def filtered(count):
        tiles = []
        for side in range(2):
            lanes = slice(128 * side, 128 * side + 128)
            total = tap_rows[0][side] * proj[8 : 8 + count, lanes]
            total = total + tap_rows[1][side] * (proj[7 : 7 + count, lanes] * lag_one[0:count, :])
            total = total + tap_rows[2][side] * (proj[6 : 6 + count, lanes] * lag_two[0:count, :])
            tiles.append(total)
        turned = pltpu.roll(tiles[0], CH, 1)
        side = is_low(count)
        return jnp.where(side, tiles[0], turned), jnp.where(side, turned, tiles[0]) * tiles[1]

    query_part, product_part = filtered(ROWS)
    query[...] = query_part
    product[...] = product_part

    offset = down - CENTER
    for g in range(PAIRS):
        lanes = slice(128 * g, 128 * g + 128)
        exponent = offset * rate[g : g + 1, :]
        value = jnp.exp(exponent) * product_part
        high = value.astype(BF16)
        weighted[0:ROWS, lanes] = high
        weighted[ROWS : 2 * ROWS, lanes] = (value - high.astype(F32)).astype(BF16)
        growth[:, lanes] = weight[g : g + 1, :] * jnp.exp(-exponent)
    last = []
    total = jnp.zeros((ROWS, 128), F32)
    for g in range(PAIRS):
        lanes = slice(128 * g, 128 * g + 128)
        inside = jnp.dot(visible[...], weighted[:, lanes], preferred_element_type=F32)
        last.append(inside[ROWS - 1 : ROWS, :])
        total = total + growth[:, lanes] * inside
    last = jnp.concatenate(last, axis=0)

    halo_copy.wait_recv()
    proj[0:8, :] = halo[...] * reach[1]
    query_top, product_top = filtered(8)
    change = product_top - product[0:8, :]
    query[0:8, :] = query_top
    product[0:8, :] = product_top
    change_zero = jnp.exp(-CENTER * rate) * change[0:1, :]
    change_one = jnp.exp((1.0 - CENTER) * rate) * change[1:2, :]
    ends[...] = jnp.exp((CENTER + 1.0 - ROWS) * rate) * (
        last + whole * (change_zero + change_one)
    )
    e_copies = []
    for k in range(3):
        copy = pltpu.make_async_remote_copy(
            src_ref=ends,
            dst_ref=incoming.at[k],
            send_sem=e_send.at[k],
            recv_sem=e_recv.at[k],
            device_id=at_y(k + 1),
            device_id_type=MESH,
        )
        copy.start()
        e_copies.append(copy)

    spread_later(EARLY + 1)

    for k in range(3):
        e_copies[k].wait_recv()
    carried = reach[1] * incoming[0]
    for k in (1, 2):
        reached = jnp.where(before[0] == before[k], reach[k + 1], 0.0)
        carried = carried + reached * jnp.exp(-float(ROWS * k) * rate) * incoming[k]
    carried = jnp.exp(-(CENTER + 1.0) * rate) * carried + change_zero
    entering = jnp.zeros((ROWS, 128), F32)
    changed = jnp.zeros((ROWS, 128), F32)
    for g in range(PAIRS):
        lanes = slice(128 * g, 128 * g + 128)
        entering = entering + growth[:, lanes] * carried[g : g + 1, :]
        changed = changed + growth[:, lanes] * change_one[g : g + 1, :]
    total = total + survives[...] * (entering + jnp.where(down >= 1.0, changed, 0.0))
    total = total + pltpu.roll(total, CH, 1)
    skips = jnp.concatenate([skip[...], skip[...]], axis=1)
    gated = query[...] * (total + skips * product[...])
    side = is_low(QUARTER)
    for h in range(2):
        top = gated[HALF * h : HALF * h + QUARTER, :]
        bottom = gated[HALF * h + QUARTER : HALF * (h + 1), :]
        a_send[h] = jnp.where(side, top, bottom).astype(BF16)

    def gather(there, target):
        return pltpu.make_async_remote_copy(
            src_ref=a_send.at[target],
            dst_ref=a_recv.at[c * nz + z],
            send_sem=as_sem.at[target * nz + there],
            recv_sem=ar_sem.at[c * nz + z],
            device_id=(y, there, x, target),
            device_id_type=MESH,
        )

    for d in range(nz - 1, 0, -1):

        @pl.when(z - d >= 0)
        def _():
            gather(z - d, c).start()
            gather(z - d, other).start()

    gather(z, other).start()
    a_recv[c * nz + z] = a_send[c]
    for d in range(1, nz):

        @pl.when(z + d < nz)
        def _():
            if d > EARLY + 1:
                wait_z(z + d, c)
            gather(z + d, c).start()
            wait_z(z + d, other)
            gather(z + d, other).start()
            if d > EARLY + 1:
                spread(z + d).start()

    def forwarded(index):
        return pltpu.make_async_remote_copy(
            src_ref=place(index, kind),
            dst_ref=place(index, kind),
            send_sem=s2_send.at[index],
            recv_sem=s2_recv.at[index],
            device_id=at_y(-1 if index % 2 else 1),
            device_id_type=MESH,
        )

    def handed(index, half):
        return pltpu.make_async_remote_copy(
            src_ref=place(index, half),
            dst_ref=place(index, half),
            send_sem=oc_send.at[2 * index + half],
            recv_sem=oc_recv.at[2 * index + half],
            device_id=(y, z, x, other),
            device_id_type=MESH,
        )

    for k in range(nz):
        pltpu.make_async_copy(place(k, kind), place(k, kind), s1_recv.at[k]).wait()

        @pl.when(z != k)
        def _():
            forwarded(k).start()

        handed(k, kind).start()
    for k in range(nz):
        pltpu.make_async_copy(place(k, 1 - kind), place(k, 1 - kind), s2_recv.at[k]).wait()
        handed(k, 1 - kind).start()

    for k in range(nz):
        for half in range(2):
            piece = wout.at[k, partner, columns(0, half)]
            pltpu.make_async_copy(piece, piece, oc_recv.at[2 * k + half]).wait()
        for h in range(2):

            @pl.when((z != k) | (c != h))
            def _():
                slot = a_recv.at[h * nz + k]
                pltpu.make_async_copy(slot, slot, ar_sem.at[h * nz + k]).wait()

        left = a_recv[k].astype(F32)
        right = a_recv[nz + k].astype(F32)
        lhs[0:QUARTER, :] = jnp.where(side, left, pltpu.roll(right, CH, 1)).astype(BF16)
        lhs[QUARTER:HALF, :] = jnp.where(side, pltpu.roll(left, CH, 1), right).astype(BF16)
        term = jnp.dot(lhs[...], wout[k], preferred_element_type=F32)
        sums[...] = term if k == 0 else sums[...] + term

    def scatter(slot, there, target):
        return pltpu.make_async_remote_copy(
            src_ref=c_send.at[slot, target],
            dst_ref=c_recv.at[c * nx + x],
            send_sem=cs_sem.at[2 * slot + target],
            recv_sem=cr_sem.at[c * nx + x],
            device_id=(y, z, there, target),
            device_id_type=MESH,
        )

    c_copies = []
    for i, d in enumerate([*distances(nx), 0]):
        there = lax.rem(x + d, nx)
        block = sums[:, pl.ds(pl.multiple_of(there * 128, 128), 128)]
        top, bottom = block[0:QUARTER, :], block[QUARTER:HALF, :]
        c_send[i, 0] = jnp.where(side, top, pltpu.roll(bottom, CH, 1)).astype(BF16)
        c_send[i, 1] = jnp.where(side, pltpu.roll(top, CH, 1), bottom).astype(BF16)
        for target in (c, other) if d else (other,):
            copy = scatter(i, there, target)
            copy.start()
            c_copies.append(copy)
    c_recv[c * nx + x] = c_send[nx - 1, c]
    for d in range(1, 2 * nx):
        sender = lax.rem(c * nx + x + d, 2 * nx)
        pltpu.make_async_copy(c_recv.at[0], c_recv.at[0], cr_sem.at[sender]).wait()
    pieces = []
    for h in range(2):
        added = c_recv[h * nx].astype(F32)
        for k in range(1, nx):
            added = added + c_recv[h * nx + k].astype(F32)
        pieces += [added, pltpu.roll(added, CH, 1)]
    result = jnp.concatenate(pieces, axis=0)
    out[...] = result.T[0:CH, :].astype(BF16)

    for copy in (*e_copies, *c_copies, halo_copy, gather(z, other)):
        copy.wait_send()
    for k in range(nz):
        handed(k, 0).wait_send()
        handed(k, 1).wait_send()

        @pl.when(z != k)
        def _():
            spread(k).wait_send()
            forwarded(k).wait_send()
            gather(k, c).wait_send()
            gather(k, other).wait_send()


def local(
    sizes,
    tokens, norm_gain, in_weight, short_filter, rates, residues, skip, out_weight, segment_ids,
):
    ny, nz, nx = sizes
    width = tokens.shape[1]
    turned = jnp.transpose(in_weight, (1, 2, 0)).reshape(3 * CH, width)
    vmem, hbm = pl.BlockSpec(memory_space=pltpu.VMEM), pl.BlockSpec(memory_space=pl.ANY)
    dma = pltpu.SemaphoreType.DMA
    result = pl.pallas_call(
        functools.partial(kernel, sizes),
        out_shape=jax.ShapeDtypeStruct((CH, ROWS), BF16),
        in_specs=[hbm] * 9,
        out_specs=vmem,
        scratch_shapes=[
            pltpu.VMEM((1, WIDTH), F32),
            pltpu.VMEM(short_filter.shape, F32),
            pltpu.VMEM(rates.shape, F32),
            pltpu.VMEM(residues.shape, F32),
            pltpu.VMEM((1, CH), F32),
            pltpu.VMEM((segment_ids.shape[0] // 128, 128), jnp.int32),
            dma((6,)),
            pltpu.VMEM((ROWS, WIDTH), BF16),
            pltpu.VMEM((3 * CH, WIDTH), BF16),
            pltpu.VMEM((nz, 2 * CH, nx * 128), BF16),
            pltpu.VMEM((ROWS + 8, 256), F32),
            pltpu.VMEM((8, 256), F32),
            pltpu.VMEM((ROWS, PAIRS * 128), F32),
            pltpu.VMEM((2 * ROWS, PAIRS * 128), BF16),
            pltpu.VMEM((ROWS, 2 * ROWS), BF16),
            pltpu.VMEM((ROWS, 128), F32),
            pltpu.VMEM((ROWS, 128), F32),
            pltpu.VMEM((ROWS, 3 * CH), F32),
            pltpu.VMEM((ROWS, 128), F32),
            pltpu.VMEM((ROWS, 128), F32),
            pltpu.VMEM((ROWS, 128), F32),
            pltpu.VMEM((PAIRS, 128), F32),
            pltpu.VMEM((3, PAIRS, 128), F32),
            pltpu.VMEM((2, QUARTER, 128), BF16),
            pltpu.VMEM((2 * nz, QUARTER, 128), BF16),
            pltpu.VMEM((HALF, 2 * CH), BF16),
            pltpu.VMEM((HALF, nx * 128), F32),
            pltpu.VMEM((nx, 2, QUARTER, 128), BF16),
            pltpu.VMEM((2 * nx, QUARTER, 128), BF16),
            dma((WIDTH // TOKEN_CHUNK,)),
            dma((WIDTH // WEIGHT_CHUNK,)),
            dma((nz,)),
            dma((nz,)),
            dma((nz,)),
            dma((nz,)),
            dma((2 * nz,)),
            dma((2 * nz,)),
            dma((2,)),
            dma((3,)),
            dma((3,)),
            dma((2 * nz,)),
            dma((2 * nz,)),
            dma((2 * nx,)),
            dma((2 * nx,)),
            pltpu.SemaphoreType.REGULAR((2 * nz,)),
        ],
        compiler_params=pltpu.CompilerParams(
            collective_id=0, has_side_effects=True, vmem_limit_bytes=60 * 1024 * 1024
        ),
    )(
        tokens,
        norm_gain.reshape(1, width),
        turned,
        short_filter,
        rates,
        residues,
        skip.reshape(1, CH),
        out_weight,
        segment_ids.reshape(-1, 128),
    )
    return result.T


def solution(mesh):
    ny = mesh.shape["ctx"]
    nz, nx = 8, 8
    torus = Mesh(mesh.devices.reshape(ny, nz, nx, 2), ("ctx", *MP))
    placed = (
        P("ctx", None),
        P(),
        P(None, None, MP),
        P(None, None, MP),
        P(None, MP),
        P(None, MP),
        P(MP),
        P(MP, None),
        P(),
    )
    return jax.shard_map(
        functools.partial(local, (ny, nz, nx)),
        mesh=torus,
        in_specs=placed,
        out_specs=P("ctx", MP),
        check_vma=False,
    )
```

```python
import functools

import jax
import jax.numpy as jnp
from jax import lax
from jax.experimental import pallas as pl
from jax.experimental.pallas import tpu as pltpu
from jax.sharding import Mesh
from jax.sharding import PartitionSpec as P

MP = ("mp_0", "mp_1", "mp_2")
MESH = pl.DeviceIdType.MESH
F32 = jnp.float32
BF16 = jnp.bfloat16

epsilon = 1e-06

ROWS = 192
HALF = ROWS // 2
QUARTER = HALF // 2
CH = 64
POLES = 16
PAIRS = POLES // 2
WIDTH = 8192
DOCS = 8
CENTER = float(ROWS // 2)
REACH = 3
SHARES = 4
EARLY = 2
TOKEN_CHUNK = 2048
WEIGHT_CHUNK = 1024


def distances(count):
    return sorted(range(1, count), key=lambda d: -min(d, count - d))


def kernel(
    sizes,
    tokens, gain_in, in_weight, taps_in, rates_in, residues_in, skip_in, out_weight, ids_in,
    out,
    gain, taps, rates, residues, skip, ids, small_sem,
    tok, win, wout, proj, halo, growth, weighted, visible, product, query, acc,
    lag_one, lag_two, survives, ends, incoming, a_send, a_recv, lhs, sums, c_send, c_recv,
    tok_sem, win_sem, s1_send, s1_recv, s2_send, s2_recv, oc_send, oc_recv,
    halo_sem, e_send, e_recv, as_sem, ar_sem, cs_sem, cr_sem, z_ready,
):
    ny, nz, nx = sizes
    y, z, x, c = (lax.axis_index(name) for name in ("ctx", *MP))
    other = 1 - c
    def at_y(step):
        return (lax.rem(y + step + ny, ny), z, x, c)

    def waited(ref, sem):
        pltpu.make_async_copy(ref, ref, sem).wait()

    small = [
        pltpu.make_async_copy(source, target, small_sem.at[k])
        for k, (source, target) in enumerate(
            (
                (ids_in, ids),
                (rates_in, rates),
                (residues_in, residues),
                (taps_in, taps),
                (skip_in, skip),
                (gain_in, gain),
            )
        )
    ]
    for load in small:
        load.start()
    tok_loads = []
    for k in range(WIDTH // TOKEN_CHUNK):
        span = pl.ds(k * TOKEN_CHUNK, TOKEN_CHUNK)
        load = pltpu.make_async_copy(tokens.at[:, span], tok.at[:, span], tok_sem.at[k])
        load.start()
        tok_loads.append(load)

    barrier = pltpu.get_barrier_semaphore()
    greeted = [(y, z, x, other)]
    for side in (c, other):
        greeted += [(y, z, lax.rem(x + d, nx), side) for d in range(1, nx)]
    steps = sorted({d % ny for k in range(1, REACH + 1) for d in (k, -k)})
    greeted += [at_y(d) for d in steps]
    for device in greeted:
        pl.semaphore_signal(barrier, inc=1, device_id=device, device_id_type=MESH)
    for d in range(1, nz):

        @pl.when(z + d < nz)
        def _():
            for side in (c, other):
                target = (y, z + d, x, side)
                pl.semaphore_signal(barrier, inc=1, device_id=target, device_id_type=MESH)

    win_loads = []
    for k in range(WIDTH // WEIGHT_CHUNK):
        span = pl.ds(k * WEIGHT_CHUNK, WEIGHT_CHUNK)
        load = pltpu.make_async_copy(in_weight.at[:, span], win.at[:, span], win_sem.at[k])
        load.start()
        win_loads.append(load)
    for load in small:
        load.wait()

    id_values = ids[...].astype(F32)
    bounds = [
        jnp.sum(jnp.where(id_values < float(k), 1.0, 0.0), axis=(0, 1), keepdims=True)
        for k in range(1, DOCS)
    ]

    def document(position):
        total = jnp.zeros_like(position)
        for bound in bounds:
            total = total + jnp.where(position >= bound, 1.0, 0.0)
        return total

    base = (y * ROWS).astype(F32)
    down = lax.broadcasted_iota(jnp.int32, (ROWS, 128), 0).astype(F32)
    own = document(down + base)

    def document_at(offset):
        return document(jnp.zeros((1, 128), F32) + (base + float(offset)))

    before = [document_at(-1 - ROWS * k) for k in range(3)]
    reach = [jnp.where(y >= k, 1.0, 0.0).astype(F32) for k in range(4)]
    survives[...] = jnp.where(own == before[0], reach[1], 0.0)
    lag_one[...] = jnp.where(own == document(down + (base - 1.0)), 1.0, 0.0)
    lag_two[...] = jnp.where(own == document(down + (base - 2.0)), 1.0, 0.0)
    whole = jnp.where(document_at(0) == document_at(ROWS - 1), 1.0, 0.0)
    across = lax.broadcasted_iota(jnp.int32, (1, 2 * ROWS), 1).astype(F32)
    across = jnp.where(across < float(ROWS), across, across - float(ROWS))
    beside = document(across + base)
    seen = (down[:, :1] >= across) & (own[:, :1] == beside)
    visible[...] = jnp.where(seen, 1.0, 0.0).astype(BF16)

    def paired(ref):
        return jnp.concatenate([ref[0:PAIRS, :], ref[PAIRS:POLES, :]], axis=1)

    rate = paired(rates)
    twice = -2.0 * rate
    small = twice * (1.0 + twice * (0.5 + twice * (1.0 / 6.0 + twice * (1.0 / 24.0 + twice * (
        1.0 / 120.0)))))
    weight = paired(residues) * jnp.sqrt(-small)

    squares = jnp.zeros((ROWS, 128), F32)
    for k in range(WIDTH // TOKEN_CHUNK):
        tok_loads[k].wait()
        for lane in range(k * TOKEN_CHUNK, (k + 1) * TOKEN_CHUNK, 128):
            piece = tok[:, lane : lane + 128].astype(F32)
            squares = squares + piece * piece
    mean_square = jnp.sum(squares, axis=1, keepdims=True) * (1.0 / WIDTH)
    scale = lax.rsqrt(mean_square + epsilon)

    pl.semaphore_wait(barrier, len(greeted) + 2 * z)
    for d in range(1, nz):

        @pl.when(z - d >= 0)
        def _():
            for side in (c, other):
                target = (y, z - d, x, side)
                pl.semaphore_signal(
                    z_ready.at[c * nz + z], inc=1, device_id=target, device_id_type=MESH
                )

    mine = pl.ds(pl.multiple_of(c * CH, CH), CH)
    partner = pl.ds(pl.multiple_of(other * CH, CH), CH)

    width = nx * 128 // SHARES
    kind = lax.rem(y, SHARES)

    def columns(there, part):
        return pl.ds(pl.multiple_of((SHARES * there + part) * width, width), width)

    def share(turned):
        return lax.rem(kind + turned + SHARES, SHARES)

    def place(index, part):
        return wout.at[index, mine, columns(0, part)]

    def spread(there):
        return pltpu.make_async_remote_copy(
            src_ref=out_weight.at[:, columns(there, kind)],
            dst_ref=place(z, kind),
            send_sem=s1_send,
            recv_sem=s1_recv.at[z],
            device_id=(y, there, x, c),
            device_id_type=MESH,
        )

    left_in, right_in, far_in = (s2_recv.at[k] for k in range(3))
    for part, sem in (
        (kind, s1_recv), (share(-1), left_in), (share(1), right_in), (share(2), far_in)
    ):
        pltpu.make_async_copy(
            out_weight.at[:, columns(z, part)], place(z, part), sem.at[z]
        ).start()
    for d in range(nz - 1, 0, -1):

        @pl.when(z - d >= 0)
        def _():
            spread(z - d).start()

    def wait_z(there, side):
        pl.semaphore_wait(z_ready.at[side * nz + there], 1)

    def spread_later(d):
        @pl.when(z + d < nz)
        def _():
            wait_z(z + d, c)
            spread(z + d).start()

    acc[...] = jnp.zeros_like(acc)
    for k in range(WIDTH // WEIGHT_CHUNK):
        win_loads[k].wait()
        span = pl.ds(k * WEIGHT_CHUNK, WEIGHT_CHUNK)
        normed = (tok[:, span].astype(F32) * scale * gain[:, span]).astype(BF16)
        acc[...] += lax.dot_general(
            normed, win[:, span], (((1,), (1,)), ((), ())), preferred_element_type=F32
        )
    proj[0:8, :] = jnp.zeros((8, 256), F32)
    rounded = acc[...].astype(BF16).astype(F32)
    proj[8 : 8 + ROWS, 0:128] = rounded[:, 0:128]
    value_part = rounded[:, 128 : 3 * CH]
    proj[8 : 8 + ROWS, 128:256] = jnp.concatenate([value_part, value_part], axis=1)
    halo_copy = pltpu.make_async_remote_copy(
        src_ref=proj.at[pl.ds(ROWS, 8)],
        dst_ref=halo,
        send_sem=halo_sem.at[0],
        recv_sem=halo_sem.at[1],
        device_id=at_y(1),
        device_id_type=MESH,
    )
    halo_copy.start()

    for d in range(1, EARLY + 1):
        spread_later(d)

    def is_low(count):
        return lax.broadcasted_iota(jnp.int32, (count, 128), 1) < CH

    tap_rows = []
    for j in range(3):
        first = jnp.concatenate([taps[j, 0:1, :], taps[j, 1:2, :]], axis=1)
        second = jnp.concatenate([taps[j, 2:3, :], taps[j, 2:3, :]], axis=1)
        tap_rows.append((first, second))

    def filtered(count):
        tiles = []
        for side in range(2):
            lanes = slice(128 * side, 128 * side + 128)
            total = tap_rows[0][side] * proj[8 : 8 + count, lanes]
            total = total + tap_rows[1][side] * (proj[7 : 7 + count, lanes] * lag_one[0:count, :])
            total = total + tap_rows[2][side] * (proj[6 : 6 + count, lanes] * lag_two[0:count, :])
            tiles.append(total)
        turned = pltpu.roll(tiles[0], CH, 1)
        side = is_low(count)
        return jnp.where(side, tiles[0], turned), jnp.where(side, turned, tiles[0]) * tiles[1]

    query_part, product_part = filtered(ROWS)
    query[...] = query_part
    product[...] = product_part

    offset = down - CENTER
    for g in range(PAIRS):
        lanes = slice(128 * g, 128 * g + 128)
        exponent = offset * rate[g : g + 1, :]
        value = jnp.exp(exponent) * product_part
        high = value.astype(BF16)
        weighted[0:ROWS, lanes] = high
        weighted[ROWS : 2 * ROWS, lanes] = (value - high.astype(F32)).astype(BF16)
        growth[:, lanes] = weight[g : g + 1, :] * jnp.exp(-exponent)
    last = []
    total = jnp.zeros((ROWS, 128), F32)
    for g in range(PAIRS):
        lanes = slice(128 * g, 128 * g + 128)
        inside = jnp.dot(visible[...], weighted[:, lanes], preferred_element_type=F32)
        last.append(inside[ROWS - 1 : ROWS, :])
        total = total + growth[:, lanes] * inside
    last = jnp.concatenate(last, axis=0)

    halo_copy.wait_recv()
    proj[0:8, :] = halo[...] * reach[1]
    query_top, product_top = filtered(8)
    change = product_top - product[0:8, :]
    query[0:8, :] = query_top
    product[0:8, :] = product_top
    change_zero = jnp.exp(-CENTER * rate) * change[0:1, :]
    change_one = jnp.exp((1.0 - CENTER) * rate) * change[1:2, :]
    ends[...] = jnp.exp((CENTER + 1.0 - ROWS) * rate) * (
        last + whole * (change_zero + change_one)
    )
    e_copies = []
    for k in range(3):
        copy = pltpu.make_async_remote_copy(
            src_ref=ends,
            dst_ref=incoming.at[k],
            send_sem=e_send.at[k],
            recv_sem=e_recv.at[k],
            device_id=at_y(k + 1),
            device_id_type=MESH,
        )
        copy.start()
        e_copies.append(copy)

    spread_later(EARLY + 1)

    for k in range(3):
        e_copies[k].wait_recv()
    carried = reach[1] * incoming[0]
    for k in (1, 2):
        reached = jnp.where(before[0] == before[k], reach[k + 1], 0.0)
        carried = carried + reached * jnp.exp(-float(ROWS * k) * rate) * incoming[k]
    carried = jnp.exp(-(CENTER + 1.0) * rate) * carried + change_zero
    entering = jnp.zeros((ROWS, 128), F32)
    changed = jnp.zeros((ROWS, 128), F32)
    for g in range(PAIRS):
        lanes = slice(128 * g, 128 * g + 128)
        entering = entering + growth[:, lanes] * carried[g : g + 1, :]
        changed = changed + growth[:, lanes] * change_one[g : g + 1, :]
    total = total + survives[...] * (entering + jnp.where(down >= 1.0, changed, 0.0))
    total = total + pltpu.roll(total, CH, 1)
    skips = jnp.concatenate([skip[...], skip[...]], axis=1)
    gated = query[...] * (total + skips * product[...])
    side = is_low(QUARTER)
    for h in range(2):
        top = gated[HALF * h : HALF * h + QUARTER, :]
        bottom = gated[HALF * h + QUARTER : HALF * (h + 1), :]
        a_send[h] = jnp.where(side, top, bottom).astype(BF16)

    def gather(there, target):
        return pltpu.make_async_remote_copy(
            src_ref=a_send.at[target],
            dst_ref=a_recv.at[c * nz + z],
            send_sem=as_sem,
            recv_sem=ar_sem.at[c * nz + z],
            device_id=(y, there, x, target),
            device_id_type=MESH,
        )

    for d in range(nz - 1, 0, -1):

        @pl.when(z - d >= 0)
        def _():
            gather(z - d, c).start()
            gather(z - d, other).start()

    gather(z, other).start()
    a_recv[c * nz + z] = a_send[c]
    for d in range(1, nz):

        @pl.when(z + d < nz)
        def _():
            if d > EARLY + 1:
                wait_z(z + d, c)
            gather(z + d, c).start()
            wait_z(z + d, other)
            gather(z + d, other).start()
            if d > EARLY + 1:
                spread(z + d).start()

    def forwarded(index, part, route):
        return pltpu.make_async_remote_copy(
            src_ref=place(index, part),
            dst_ref=place(index, part),
            send_sem=s2_send,
            recv_sem=s2_recv.at[route, index],
            device_id=at_y(-1 if route == 1 or (route == 2 and index % 2) else 1),
            device_id_type=MESH,
        )

    def relayed(index):
        return forwarded(index, share(1 if index % 2 else -1), 2)

    def handed(index, part):
        return pltpu.make_async_remote_copy(
            src_ref=place(index, part),
            dst_ref=place(index, part),
            send_sem=oc_send,
            recv_sem=oc_recv.at[index],
            device_id=(y, z, x, other),
            device_id_type=MESH,
        )

    def arrived(index, part, sem):
        pltpu.make_async_copy(place(index, part), place(index, part), sem.at[index]).wait()

    def summed(k):
        pltpu.make_async_copy(wout.at[k, partner], wout.at[k, partner], oc_recv.at[k]).wait()
        for h in range(2):

            @pl.when((z != k) | (c != h))
            def _():
                slot = a_recv.at[h * nz + k]
                pltpu.make_async_copy(slot, slot, ar_sem.at[h * nz + k]).wait()

        left = a_recv[k].astype(F32)
        right = a_recv[nz + k].astype(F32)
        lhs[0:QUARTER, :] = jnp.where(side, left, pltpu.roll(right, CH, 1)).astype(BF16)
        lhs[QUARTER:HALF, :] = jnp.where(side, pltpu.roll(left, CH, 1), right).astype(BF16)
        term = jnp.dot(lhs[...], wout[k], preferred_element_type=F32)
        sums[...] = term if k == 0 else sums[...] + term

    for k in range(nz):
        arrived(k, kind, s1_recv)

        @pl.when(z != k)
        def _():
            forwarded(k, kind, 0).start()
            forwarded(k, kind, 1).start()

        handed(k, kind).start()
    for k in range(nz):
        arrived(k, share(-1), left_in)
        arrived(k, share(1), right_in)

        @pl.when(z != k)
        def _():
            relayed(k).start()

        handed(k, share(-1)).start()
        handed(k, share(1)).start()
    for k in range(nz):
        arrived(k, share(2), far_in)
        handed(k, share(2)).start()
        if k >= 2:
            summed(k - 2)
    summed(nz - 2)
    summed(nz - 1)

    def scatter(slot, there, target):
        return pltpu.make_async_remote_copy(
            src_ref=c_send.at[slot, target],
            dst_ref=c_recv.at[c * nx + x],
            send_sem=cs_sem,
            recv_sem=cr_sem,
            device_id=(y, z, there, target),
            device_id_type=MESH,
        )

    for i, d in enumerate([*distances(nx), 0]):
        there = lax.rem(x + d, nx)
        block = sums[:, pl.ds(pl.multiple_of(there * 128, 128), 128)]
        top, bottom = block[0:QUARTER, :], block[QUARTER:HALF, :]
        c_send[i, 0] = jnp.where(side, top, pltpu.roll(bottom, CH, 1)).astype(BF16)
        c_send[i, 1] = jnp.where(side, pltpu.roll(top, CH, 1), bottom).astype(BF16)
        for target in (c, other) if d else (other,):
            scatter(i, there, target).start()
    c_recv[c * nx + x] = c_send[nx - 1, c]
    waited(c_recv.at[pl.ds(0, 2 * nx - 1)], cr_sem)
    pieces = []
    for h in range(2):
        added = c_recv[h * nx].astype(F32)
        for k in range(1, nx):
            added = added + c_recv[h * nx + k].astype(F32)
        pieces += [added, pltpu.roll(added, CH, 1)]
    result = jnp.concatenate(pieces, axis=0)
    out[...] = result.T[0:CH, :].astype(BF16)

    for copy in (*e_copies, halo_copy):
        copy.wait_send()
    rows = pl.ds(0, nz - 1)
    waited(wout.at[rows, mine, pl.ds(0, width)], s1_send)
    waited(wout.at[rows, mine, pl.ds(0, 3 * width)], s2_send)
    waited(wout.at[:, mine], oc_send)
    waited(a_recv.at[pl.ds(0, 2 * nz - 1)], as_sem)
    waited(c_recv.at[pl.ds(0, 2 * nx - 1)], cs_sem)


def local(
    sizes,
    tokens, norm_gain, in_weight, short_filter, rates, residues, skip, out_weight, segment_ids,
):
    ny, nz, nx = sizes
    width = tokens.shape[1]
    turned = jnp.transpose(in_weight, (1, 2, 0)).reshape(3 * CH, width)
    vmem, hbm = pl.BlockSpec(memory_space=pltpu.VMEM), pl.BlockSpec(memory_space=pl.ANY)
    dma = pltpu.SemaphoreType.DMA
    result = pl.pallas_call(
        functools.partial(kernel, sizes),
        out_shape=jax.ShapeDtypeStruct((CH, ROWS), BF16),
        in_specs=[hbm] * 9,
        out_specs=vmem,
        scratch_shapes=[
            pltpu.VMEM((1, WIDTH), F32),
            pltpu.VMEM(short_filter.shape, F32),
            pltpu.VMEM(rates.shape, F32),
            pltpu.VMEM(residues.shape, F32),
            pltpu.VMEM((1, CH), F32),
            pltpu.VMEM((segment_ids.shape[0] // 128, 128), jnp.int32),
            dma((6,)),
            pltpu.VMEM((ROWS, WIDTH), BF16),
            pltpu.VMEM((3 * CH, WIDTH), BF16),
            pltpu.VMEM((nz, 2 * CH, nx * 128), BF16),
            pltpu.VMEM((ROWS + 8, 256), F32),
            pltpu.VMEM((8, 256), F32),
            pltpu.VMEM((ROWS, PAIRS * 128), F32),
            pltpu.VMEM((2 * ROWS, PAIRS * 128), BF16),
            pltpu.VMEM((ROWS, 2 * ROWS), BF16),
            pltpu.VMEM((ROWS, 128), F32),
            pltpu.VMEM((ROWS, 128), F32),
            pltpu.VMEM((ROWS, 3 * CH), F32),
            pltpu.VMEM((ROWS, 128), F32),
            pltpu.VMEM((ROWS, 128), F32),
            pltpu.VMEM((ROWS, 128), F32),
            pltpu.VMEM((PAIRS, 128), F32),
            pltpu.VMEM((3, PAIRS, 128), F32),
            pltpu.VMEM((2, QUARTER, 128), BF16),
            pltpu.VMEM((2 * nz, QUARTER, 128), BF16),
            pltpu.VMEM((HALF, 2 * CH), BF16),
            pltpu.VMEM((HALF, nx * 128), F32),
            pltpu.VMEM((nx, 2, QUARTER, 128), BF16),
            pltpu.VMEM((2 * nx, QUARTER, 128), BF16),
            dma((WIDTH // TOKEN_CHUNK,)),
            dma((WIDTH // WEIGHT_CHUNK,)),
            dma,
            dma((nz,)),
            dma,
            dma((3, nz)),
            dma,
            dma((nz,)),
            dma((2,)),
            dma((3,)),
            dma((3,)),
            dma,
            dma((2 * nz,)),
            dma,
            dma,
            pltpu.SemaphoreType.REGULAR((2 * nz,)),
        ],
        compiler_params=pltpu.CompilerParams(
            collective_id=0, has_side_effects=True, vmem_limit_bytes=60 * 1024 * 1024
        ),
    )(
        tokens,
        norm_gain.reshape(1, width),
        turned,
        short_filter,
        rates,
        residues,
        skip.reshape(1, CH),
        out_weight,
        segment_ids.reshape(-1, 128),
    )
    return result.T


def solution(mesh):
    ny = mesh.shape["ctx"]
    nz, nx = 8, 8
    torus = Mesh(mesh.devices.reshape(ny, nz, nx, 2), ("ctx", *MP))
    placed = (
        P("ctx", None),
        P(),
        P(None, None, MP),
        P(None, None, MP),
        P(None, MP),
        P(None, MP),
        P(MP),
        P(MP, None),
        P(),
    )
    return jax.shard_map(
        functools.partial(local, (ny, nz, nx)),
        mesh=torus,
        in_specs=placed,
        out_specs=P("ctx", MP),
        check_vma=False,
    )
```

```python
import functools

import jax
import jax.numpy as jnp
from jax import lax
from jax.experimental import pallas as pl
from jax.experimental.pallas import tpu as pltpu
from jax.sharding import Mesh
from jax.sharding import PartitionSpec as P

MP = ("mp_0", "mp_1", "mp_2")
MESH = pl.DeviceIdType.MESH
F32 = jnp.float32
BF16 = jnp.bfloat16

epsilon = 1e-06

ROWS = 192
HALF = ROWS // 2
QUARTER = HALF // 2
CH = 64
POLES = 16
PAIRS = POLES // 2
WIDTH = 8192
DOCS = 8
CENTER = float(ROWS // 2)
REACH = 3
SHARES = 4
EARLY = 2
TOKEN_CHUNK = 2048
WEIGHT_CHUNK = 1024


def distances(count):
    return sorted(range(1, count), key=lambda d: -min(d, count - d))


def kernel(
    sizes,
    tokens, gain_in, in_weight, taps_in, rates_in, residues_in, skip_in, out_weight, ids_in,
    out,
    gain, taps, rates, residues, skip, ids, small_sem,
    tok, win, wout, proj, halo, growth, weighted, visible, product, query, acc,
    lag_one, lag_two, survives, ends, incoming, carry, a_send, a_recv, lhs, sums, c_send, c_recv,
    tok_sem, win_sem, s1_send, s1_recv, s2_send, s2_recv, oc_send, oc_recv,
    halo_sem, e_send, e_recv, as_sem, ar_sem, cs_sem, cr_sem, z_ready,
):
    ny, nz, nx = sizes
    y, z, x, c = (lax.axis_index(name) for name in ("ctx", *MP))
    other = 1 - c
    def at_y(step):
        return (lax.rem(y + step + ny, ny), z, x, c)

    def waited(ref, sem):
        pltpu.make_async_copy(ref, ref, sem).wait()

    small = [
        pltpu.make_async_copy(source, target, small_sem.at[k])
        for k, (source, target) in enumerate(
            (
                (ids_in, ids),
                (rates_in, rates),
                (residues_in, residues),
                (taps_in, taps),
                (skip_in, skip),
                (gain_in, gain),
            )
        )
    ]
    for load in small:
        load.start()
    tok_loads = []
    for k in range(WIDTH // TOKEN_CHUNK):
        span = pl.ds(k * TOKEN_CHUNK, TOKEN_CHUNK)
        load = pltpu.make_async_copy(tokens.at[:, span], tok.at[:, span], tok_sem.at[k])
        load.start()
        tok_loads.append(load)

    barrier = pltpu.get_barrier_semaphore()
    greeted = [(y, z, x, other)]
    for side in (c, other):
        greeted += [(y, z, lax.rem(x + d, nx), side) for d in range(1, nx)]
    steps = sorted({d % ny for k in range(1, REACH + 1) for d in (k, -k)})
    greeted += [at_y(d) for d in steps]
    for device in greeted:
        pl.semaphore_signal(barrier, inc=1, device_id=device, device_id_type=MESH)
    for d in range(1, nz):

        @pl.when(z + d < nz)
        def _():
            for side in (c, other):
                target = (y, z + d, x, side)
                pl.semaphore_signal(barrier, inc=1, device_id=target, device_id_type=MESH)

    win_loads = []
    for k in range(WIDTH // WEIGHT_CHUNK):
        span = pl.ds(k * WEIGHT_CHUNK, WEIGHT_CHUNK)
        load = pltpu.make_async_copy(in_weight.at[:, span], win.at[:, span], win_sem.at[k])
        load.start()
        win_loads.append(load)
    for load in small:
        load.wait()

    id_values = ids[...].astype(F32)
    bounds = [
        jnp.sum(jnp.where(id_values < float(k), 1.0, 0.0), axis=(0, 1), keepdims=True)
        for k in range(1, DOCS)
    ]

    def document(position):
        total = jnp.zeros_like(position)
        for bound in bounds:
            total = total + jnp.where(position >= bound, 1.0, 0.0)
        return total

    base = (y * ROWS).astype(F32)
    down = lax.broadcasted_iota(jnp.int32, (ROWS, 128), 0).astype(F32)
    own = document(down + base)

    def document_at(offset):
        return document(jnp.zeros((1, 128), F32) + (base + float(offset)))

    before = [document_at(-1 - ROWS * k) for k in range(3)]
    reach = [jnp.where(y >= k, 1.0, 0.0).astype(F32) for k in range(4)]
    survives[...] = jnp.where(own == before[0], reach[1], 0.0)
    lag_one[...] = jnp.where(own == document(down + (base - 1.0)), 1.0, 0.0)
    lag_two[...] = jnp.where(own == document(down + (base - 2.0)), 1.0, 0.0)
    whole = jnp.where(document_at(0) == document_at(ROWS - 1), 1.0, 0.0)
    across = lax.broadcasted_iota(jnp.int32, (1, 2 * ROWS), 1).astype(F32)
    across = jnp.where(across < float(ROWS), across, across - float(ROWS))
    beside = document(across + base)
    seen = (down[:, :1] >= across) & (own[:, :1] == beside)
    visible[...] = jnp.where(seen, 1.0, 0.0).astype(BF16)

    def paired(ref):
        return jnp.concatenate([ref[0:PAIRS, :], ref[PAIRS:POLES, :]], axis=1)

    rate = paired(rates)
    twice = -2.0 * rate
    small = twice * (1.0 + twice * (0.5 + twice * (1.0 / 6.0 + twice * (1.0 / 24.0 + twice * (
        1.0 / 120.0)))))
    weight = paired(residues) * jnp.sqrt(-small)

    squares = jnp.zeros((ROWS, 128), F32)
    for k in range(WIDTH // TOKEN_CHUNK):
        tok_loads[k].wait()
        for lane in range(k * TOKEN_CHUNK, (k + 1) * TOKEN_CHUNK, 128):
            piece = tok[:, lane : lane + 128].astype(F32)
            squares = squares + piece * piece
    mean_square = jnp.sum(squares, axis=1, keepdims=True) * (1.0 / WIDTH)
    scale = lax.rsqrt(mean_square + epsilon)

    pl.semaphore_wait(barrier, len(greeted) + 2 * z)
    for d in range(1, nz):

        @pl.when(z - d >= 0)
        def _():
            for side in (c, other):
                target = (y, z - d, x, side)
                pl.semaphore_signal(
                    z_ready.at[c * nz + z], inc=1, device_id=target, device_id_type=MESH
                )

    mine = pl.ds(pl.multiple_of(c * CH, CH), CH)
    partner = pl.ds(pl.multiple_of(other * CH, CH), CH)

    width = nx * 128 // SHARES
    kind = lax.rem(y, SHARES)

    def columns(there, part):
        return pl.ds(pl.multiple_of((SHARES * there + part) * width, width), width)

    def share(turned):
        return lax.rem(kind + turned + SHARES, SHARES)

    def place(index, part):
        return wout.at[index, mine, columns(0, part)]

    def spread(there):
        return pltpu.make_async_remote_copy(
            src_ref=out_weight.at[:, columns(there, kind)],
            dst_ref=place(z, kind),
            send_sem=s1_send,
            recv_sem=s1_recv.at[z],
            device_id=(y, there, x, c),
            device_id_type=MESH,
        )

    left_in, right_in, far_in = (s2_recv.at[k] for k in range(3))
    for part, sem in (
        (kind, s1_recv), (share(-1), left_in), (share(1), right_in), (share(2), far_in)
    ):
        pltpu.make_async_copy(
            out_weight.at[:, columns(z, part)], place(z, part), sem.at[z]
        ).start()
    for d in range(nz - 1, 0, -1):

        @pl.when(z - d >= 0)
        def _():
            spread(z - d).start()

    def wait_z(there, side):
        pl.semaphore_wait(z_ready.at[side * nz + there], 1)

    def spread_later(d):
        @pl.when(z + d < nz)
        def _():
            wait_z(z + d, c)
            spread(z + d).start()

    acc[...] = jnp.zeros_like(acc)
    for k in range(WIDTH // WEIGHT_CHUNK):
        win_loads[k].wait()
        span = pl.ds(k * WEIGHT_CHUNK, WEIGHT_CHUNK)
        normed = (tok[:, span].astype(F32) * scale * gain[:, span]).astype(BF16)
        acc[...] += lax.dot_general(
            normed, win[:, span], (((1,), (1,)), ((), ())), preferred_element_type=F32
        )
    proj[0:8, :] = jnp.zeros((8, 256), F32)
    rounded = acc[...].astype(BF16).astype(F32)
    proj[8 : 8 + ROWS, 0:128] = rounded[:, 0:128]
    value_part = rounded[:, 128 : 3 * CH]
    proj[8 : 8 + ROWS, 128:256] = jnp.concatenate([value_part, value_part], axis=1)
    def send_halo():
        return pltpu.make_async_remote_copy(
            src_ref=proj.at[pl.ds(ROWS, 8)],
            dst_ref=halo,
            send_sem=halo_sem.at[0],
            recv_sem=halo_sem.at[1],
            device_id=at_y(1),
            device_id_type=MESH,
        )

    @pl.when(y + 1 < ny)
    def _():
        send_halo().start()

    for d in range(1, EARLY + 1):
        spread_later(d)

    def is_low(count):
        return lax.broadcasted_iota(jnp.int32, (count, 128), 1) < CH

    tap_rows = []
    for j in range(3):
        first = jnp.concatenate([taps[j, 0:1, :], taps[j, 1:2, :]], axis=1)
        second = jnp.concatenate([taps[j, 2:3, :], taps[j, 2:3, :]], axis=1)
        tap_rows.append((first, second))

    def filtered(count):
        tiles = []
        for side in range(2):
            lanes = slice(128 * side, 128 * side + 128)
            total = tap_rows[0][side] * proj[8 : 8 + count, lanes]
            total = total + tap_rows[1][side] * (proj[7 : 7 + count, lanes] * lag_one[0:count, :])
            total = total + tap_rows[2][side] * (proj[6 : 6 + count, lanes] * lag_two[0:count, :])
            tiles.append(total)
        turned = pltpu.roll(tiles[0], CH, 1)
        side = is_low(count)
        return jnp.where(side, tiles[0], turned), jnp.where(side, turned, tiles[0]) * tiles[1]

    query_part, product_part = filtered(ROWS)
    query[...] = query_part
    product[...] = product_part

    offset = down - CENTER
    for g in range(PAIRS):
        lanes = slice(128 * g, 128 * g + 128)
        exponent = offset * rate[g : g + 1, :]
        value = jnp.exp(exponent) * product_part
        high = value.astype(BF16)
        weighted[0:ROWS, lanes] = high
        weighted[ROWS : 2 * ROWS, lanes] = (value - high.astype(F32)).astype(BF16)
        growth[:, lanes] = weight[g : g + 1, :] * jnp.exp(-exponent)
    last = []
    total = jnp.zeros((ROWS, 128), F32)
    for g in range(PAIRS):
        lanes = slice(128 * g, 128 * g + 128)
        inside = jnp.dot(visible[...], weighted[:, lanes], preferred_element_type=F32)
        last.append(inside[ROWS - 1 : ROWS, :])
        total = total + growth[:, lanes] * inside
    last = jnp.concatenate(last, axis=0)

    @pl.when(y >= 1)
    def _():
        waited(halo, halo_sem.at[1])
        proj[0:8, :] = halo[...]

    query_top, product_top = filtered(8)
    change = product_top - product[0:8, :]
    query[0:8, :] = query_top
    product[0:8, :] = product_top
    change_zero = jnp.exp(-CENTER * rate) * change[0:1, :]
    change_one = jnp.exp((1.0 - CENTER) * rate) * change[1:2, :]
    ends[...] = jnp.exp((CENTER + 1.0 - ROWS) * rate) * (
        last + whole * (change_zero + change_one)
    )
    def send_ends(k):
        return pltpu.make_async_remote_copy(
            src_ref=ends,
            dst_ref=incoming.at[k - 1],
            send_sem=e_send.at[k - 1],
            recv_sem=e_recv.at[k - 1],
            device_id=at_y(k),
            device_id_type=MESH,
        )

    for k in range(1, REACH + 1):

        @pl.when(y + k < ny)
        def _():
            send_ends(k).start()

    spread_later(EARLY + 1)

    carry[...] = jnp.zeros((PAIRS, 128), F32)
    for k in range(1, REACH + 1):

        @pl.when(y >= k)
        def _():
            waited(incoming.at[k - 1], e_recv.at[k - 1])
            reached = jnp.where(before[0] == before[k - 1], 1.0, 0.0)
            carry[...] += reached * jnp.exp(-float(ROWS * (k - 1)) * rate) * incoming[k - 1]

    carried = jnp.exp(-(CENTER + 1.0) * rate) * carry[...] + change_zero
    entering = jnp.zeros((ROWS, 128), F32)
    changed = jnp.zeros((ROWS, 128), F32)
    for g in range(PAIRS):
        lanes = slice(128 * g, 128 * g + 128)
        entering = entering + growth[:, lanes] * carried[g : g + 1, :]
        changed = changed + growth[:, lanes] * change_one[g : g + 1, :]
    total = total + survives[...] * (entering + jnp.where(down >= 1.0, changed, 0.0))
    total = total + pltpu.roll(total, CH, 1)
    skips = jnp.concatenate([skip[...], skip[...]], axis=1)
    gated = query[...] * (total + skips * product[...])
    side = is_low(QUARTER)
    for h in range(2):
        top = gated[HALF * h : HALF * h + QUARTER, :]
        bottom = gated[HALF * h + QUARTER : HALF * (h + 1), :]
        a_send[h] = jnp.where(side, top, bottom).astype(BF16)

    def gather(there, target):
        return pltpu.make_async_remote_copy(
            src_ref=a_send.at[target],
            dst_ref=a_recv.at[c * nz + z],
            send_sem=as_sem,
            recv_sem=ar_sem.at[c * nz + z],
            device_id=(y, there, x, target),
            device_id_type=MESH,
        )

    for d in range(nz - 1, 0, -1):

        @pl.when(z - d >= 0)
        def _():
            gather(z - d, c).start()
            gather(z - d, other).start()

    gather(z, other).start()
    a_recv[c * nz + z] = a_send[c]
    for d in range(1, nz):

        @pl.when(z + d < nz)
        def _():
            if d > EARLY + 1:
                wait_z(z + d, c)
            gather(z + d, c).start()
            wait_z(z + d, other)
            gather(z + d, other).start()
            if d > EARLY + 1:
                spread(z + d).start()

    def forwarded(index, part, route):
        return pltpu.make_async_remote_copy(
            src_ref=place(index, part),
            dst_ref=place(index, part),
            send_sem=s2_send,
            recv_sem=s2_recv.at[route, index],
            device_id=at_y(-1 if route == 1 or (route == 2 and index % 2) else 1),
            device_id_type=MESH,
        )

    def relayed(index):
        return forwarded(index, share(1 if index % 2 else -1), 2)

    def handed(index, part):
        return pltpu.make_async_remote_copy(
            src_ref=place(index, part),
            dst_ref=place(index, part),
            send_sem=oc_send,
            recv_sem=oc_recv.at[index],
            device_id=(y, z, x, other),
            device_id_type=MESH,
        )

    def arrived(index, part, sem):
        pltpu.make_async_copy(place(index, part), place(index, part), sem.at[index]).wait()

    def summed(k):
        pltpu.make_async_copy(wout.at[k, partner], wout.at[k, partner], oc_recv.at[k]).wait()
        for h in range(2):

            @pl.when((z != k) | (c != h))
            def _():
                slot = a_recv.at[h * nz + k]
                pltpu.make_async_copy(slot, slot, ar_sem.at[h * nz + k]).wait()

        left = a_recv[k].astype(F32)
        right = a_recv[nz + k].astype(F32)
        lhs[0:QUARTER, :] = jnp.where(side, left, pltpu.roll(right, CH, 1)).astype(BF16)
        lhs[QUARTER:HALF, :] = jnp.where(side, pltpu.roll(left, CH, 1), right).astype(BF16)
        term = jnp.dot(lhs[...], wout[k], preferred_element_type=F32)
        sums[...] = term if k == 0 else sums[...] + term

    for k in range(nz):
        arrived(k, kind, s1_recv)

        @pl.when(z != k)
        def _():
            forwarded(k, kind, 0).start()
            forwarded(k, kind, 1).start()

        handed(k, kind).start()
    for k in range(nz):
        arrived(k, share(-1), left_in)
        arrived(k, share(1), right_in)

        @pl.when(z != k)
        def _():
            relayed(k).start()

        handed(k, share(-1)).start()
        handed(k, share(1)).start()
    for k in range(nz):
        arrived(k, share(2), far_in)
        handed(k, share(2)).start()
        if k >= 2:
            summed(k - 2)
    summed(nz - 2)
    summed(nz - 1)

    def scatter(slot, there, target):
        return pltpu.make_async_remote_copy(
            src_ref=c_send.at[slot, target],
            dst_ref=c_recv.at[c * nx + x],
            send_sem=cs_sem,
            recv_sem=cr_sem,
            device_id=(y, z, there, target),
            device_id_type=MESH,
        )

    for i, d in enumerate([*distances(nx), 0]):
        there = lax.rem(x + d, nx)
        block = sums[:, pl.ds(pl.multiple_of(there * 128, 128), 128)]
        top, bottom = block[0:QUARTER, :], block[QUARTER:HALF, :]
        c_send[i, 0] = jnp.where(side, top, pltpu.roll(bottom, CH, 1)).astype(BF16)
        c_send[i, 1] = jnp.where(side, pltpu.roll(top, CH, 1), bottom).astype(BF16)
        for target in (c, other) if d else (other,):
            scatter(i, there, target).start()
    c_recv[c * nx + x] = c_send[nx - 1, c]
    waited(c_recv.at[pl.ds(0, 2 * nx - 1)], cr_sem)
    pieces = []
    for h in range(2):
        added = c_recv[h * nx].astype(F32)
        for k in range(1, nx):
            added = added + c_recv[h * nx + k].astype(F32)
        pieces += [added, pltpu.roll(added, CH, 1)]
    result = jnp.concatenate(pieces, axis=0)
    out[...] = result.T[0:CH, :].astype(BF16)

    @pl.when(y + 1 < ny)
    def _():
        send_halo().wait_send()

    for k in range(1, REACH + 1):

        @pl.when(y + k < ny)
        def _():
            send_ends(k).wait_send()

    rows = pl.ds(0, nz - 1)
    waited(wout.at[rows, mine, pl.ds(0, width)], s1_send)
    waited(wout.at[rows, mine, pl.ds(0, 3 * width)], s2_send)
    waited(wout.at[:, mine], oc_send)
    waited(a_recv.at[pl.ds(0, 2 * nz - 1)], as_sem)
    waited(c_recv.at[pl.ds(0, 2 * nx - 1)], cs_sem)


def local(
    sizes,
    tokens, norm_gain, in_weight, short_filter, rates, residues, skip, out_weight, segment_ids,
):
    ny, nz, nx = sizes
    width = tokens.shape[1]
    turned = jnp.transpose(in_weight, (1, 2, 0)).reshape(3 * CH, width)
    vmem, hbm = pl.BlockSpec(memory_space=pltpu.VMEM), pl.BlockSpec(memory_space=pl.ANY)
    dma = pltpu.SemaphoreType.DMA
    result = pl.pallas_call(
        functools.partial(kernel, sizes),
        out_shape=jax.ShapeDtypeStruct((CH, ROWS), BF16),
        in_specs=[hbm] * 9,
        out_specs=vmem,
        scratch_shapes=[
            pltpu.VMEM((1, WIDTH), F32),
            pltpu.VMEM(short_filter.shape, F32),
            pltpu.VMEM(rates.shape, F32),
            pltpu.VMEM(residues.shape, F32),
            pltpu.VMEM((1, CH), F32),
            pltpu.VMEM((segment_ids.shape[0] // 128, 128), jnp.int32),
            dma((6,)),
            pltpu.VMEM((ROWS, WIDTH), BF16),
            pltpu.VMEM((3 * CH, WIDTH), BF16),
            pltpu.VMEM((nz, 2 * CH, nx * 128), BF16),
            pltpu.VMEM((ROWS + 8, 256), F32),
            pltpu.VMEM((8, 256), F32),
            pltpu.VMEM((ROWS, PAIRS * 128), F32),
            pltpu.VMEM((2 * ROWS, PAIRS * 128), BF16),
            pltpu.VMEM((ROWS, 2 * ROWS), BF16),
            pltpu.VMEM((ROWS, 128), F32),
            pltpu.VMEM((ROWS, 128), F32),
            pltpu.VMEM((ROWS, 3 * CH), F32),
            pltpu.VMEM((ROWS, 128), F32),
            pltpu.VMEM((ROWS, 128), F32),
            pltpu.VMEM((ROWS, 128), F32),
            pltpu.VMEM((PAIRS, 128), F32),
            pltpu.VMEM((REACH, PAIRS, 128), F32),
            pltpu.VMEM((PAIRS, 128), F32),
            pltpu.VMEM((2, QUARTER, 128), BF16),
            pltpu.VMEM((2 * nz, QUARTER, 128), BF16),
            pltpu.VMEM((HALF, 2 * CH), BF16),
            pltpu.VMEM((HALF, nx * 128), F32),
            pltpu.VMEM((nx, 2, QUARTER, 128), BF16),
            pltpu.VMEM((2 * nx, QUARTER, 128), BF16),
            dma((WIDTH // TOKEN_CHUNK,)),
            dma((WIDTH // WEIGHT_CHUNK,)),
            dma,
            dma((nz,)),
            dma,
            dma((3, nz)),
            dma,
            dma((nz,)),
            dma((2,)),
            dma((3,)),
            dma((3,)),
            dma,
            dma((2 * nz,)),
            dma,
            dma,
            pltpu.SemaphoreType.REGULAR((2 * nz,)),
        ],
        compiler_params=pltpu.CompilerParams(
            collective_id=0, has_side_effects=True, vmem_limit_bytes=60 * 1024 * 1024
        ),
    )(
        tokens,
        norm_gain.reshape(1, width),
        turned,
        short_filter,
        rates,
        residues,
        skip.reshape(1, CH),
        out_weight,
        segment_ids.reshape(-1, 128),
    )
    return result.T


def solution(mesh):
    ny = mesh.shape["ctx"]
    nz, nx = 8, 8
    torus = Mesh(mesh.devices.reshape(ny, nz, nx, 2), ("ctx", *MP))
    placed = (
        P("ctx", None),
        P(),
        P(None, None, MP),
        P(None, None, MP),
        P(None, MP),
        P(None, MP),
        P(MP),
        P(MP, None),
        P(),
    )
    return jax.shard_map(
        functools.partial(local, (ny, nz, nx)),
        mesh=torus,
        in_specs=placed,
        out_specs=P("ctx", MP),
        check_vma=False,
    )
```
